32 devices in a mesh: tok: 2 (over x), feat: 4 (over z), pb: 4 (over y, core).
Axes of the slice: x: 2, y: 2, z: 4, core: 2. Of those that a mesh axis runs over, the one named last changes fastest.
Arguments:
- out_grads: bfloat16 [10240, 8192], P(('tok', 'pb'), 'feat'), may hold values from -6 to 6
- acts: bfloat16 [10240, 8192], P(('tok', 'pb'), 'feat'), may hold values from -6 to 6
- s_inverse: bfloat16 [8192, 8192], P('feat', ('tok', 'pb')), may hold values from -1 to 3, as said below
- a_inverse: bfloat16 [8192, 8192], P('feat', ('tok', 'pb')), may hold values from -1 to 3, as said below
- query_out: bfloat16 [8192, 512], P(('tok', 'pb')), may hold values from -0.0625 to 0.0625
- query_in: bfloat16 [8192, 512], P(('tok', 'pb')), may hold values from -0.0625 to 0.0625
Outputs:
- scores: float32 [32, 10240], P('feat', ('tok', 'pb'))
The draws below stay inside these ranges and needn't reach their ends.
Inputs may be any that keep to these rules, and one draw needn't show every extreme that they name: `s_inverse`: symmetric; diagonal entries roughly between 0.5 and 2. `a_inverse`: symmetric; diagonal entries roughly between 0.5 and 2.
All inputs are finite; a program needn't handle non-finite values.
Results may differ from the reference program's by a relative error of at most 0.0041.
Values may be sent and summed in bfloat16 or wider, within the bound.
No kernel may reach another device: no remote copies, remote signals or barrier semaphores. Data moves between devices by JAX's collectives and lax.ppermute only.
A program may use at most 128 MiB of HBM per device.

```python
import jax
import jax.numpy as jnp
from jax import lax

D = 8192
RANK = 16
QUERIES = 32
TOK_DEV = 1280
QR = 512
TOKENS = 10240


def factor_draw(key):
    first, second = jax.random.split(key)
    diag_vals = jnp.exp(jax.random.uniform(first, (D,), jnp.float32, jnp.log(0.5), jnp.log(2.0)))
    noise = jax.random.normal(second, (D, D), jnp.float32)
    symmetric = (noise + noise.T) * (0.25 / D ** 0.5)
    return (jnp.diag(diag_vals) + symmetric).astype(jnp.bfloat16)


def draw_s_inverse(key, part):
    return factor_draw(jax.random.fold_in(key, 11))


def draw_a_inverse(key, part):
    return factor_draw(jax.random.fold_in(key, 23))


def level_of(key, extent, pieces, low, high):
    factor_of = 1.0
    for axis_at, parts in pieces:
        steps = jax.random.uniform(jax.random.fold_in(jax.random.fold_in(key, 6), axis_at), (parts,), jnp.float32, low / len(pieces), high / len(pieces))
        factor_of = factor_of * jnp.repeat(jnp.exp(steps), extent[axis_at] // parts).reshape((-1,) + (1,) * (len(extent) - 1 - axis_at))
    return factor_of


def bell_draw(own_key, shape, width, reach, cuts=(), dtype=jnp.bfloat16):
    drawn = jax.random.normal(own_key, shape, jnp.float32) * width
    if len(cuts) > 0:
        drawn = level_of(own_key, shape, cuts, -0.22, 0.18) * drawn
    return jnp.clip(drawn, min=-reach, max=reach).astype(dtype)


def setup_inputs(seed: int = 0) -> dict:
    key_list = jax.random.split(jax.random.key(seed), 7)
    out_grads = bell_draw(key_list[0], (TOKENS, D), 1.0, 6.0, ((0, 8), (1, 4)))
    acts = bell_draw(key_list[1], (TOKENS, D), 1.0, 6.0, ((0, 8), (1, 4)))
    s_inverse = draw_s_inverse(jax.random.fold_in(key_list[6], 71), 0)
    a_inverse = draw_a_inverse(jax.random.fold_in(key_list[6], 71), 0)
    query_out = bell_draw(key_list[4], (D, QR), D ** -0.5, 0.0625, ((0, 8),))
    query_in = bell_draw(key_list[5], (D, QR), D ** -0.5, 0.0625, ((0, 8),))
    return dict(out_grads=out_grads, acts=acts, s_inverse=s_inverse, a_inverse=a_inverse, query_out=query_out, query_in=query_in)


def reference(out_grads, acts, s_inverse, a_inverse, query_out, query_in):
    left_pre = jnp.dot(s_inverse, query_out, preferred_element_type=jnp.float32).astype(jnp.bfloat16)
    right_pre = jnp.dot(a_inverse, query_in, preferred_element_type=jnp.float32).astype(jnp.bfloat16)
    scale = 1.0 / (RANK ** 0.5)

    def one_block(pair):
        grads, inputs = pair
        grad_proj = jnp.dot(grads, left_pre, preferred_element_type=jnp.float32)
        act_proj = jnp.dot(inputs, right_pre, preferred_element_type=jnp.float32)
        summed = (grad_proj * act_proj).reshape(grads.shape[0], QUERIES, RANK).sum(axis=2)
        return (summed * scale).T

    grads_all = out_grads.reshape(-1, TOK_DEV, D)
    inputs_all = acts.reshape(-1, TOK_DEV, D)
    blocks = lax.map(one_block, (grads_all, inputs_all))
    return jnp.transpose(blocks, (1, 0, 2)).reshape(QUERIES, TOKENS)
```

```python
import functools

import jax
import jax.numpy as jnp
import numpy as np
from jax import lax
from jax.experimental import pallas as pl
from jax.experimental.pallas import tpu as pltpu
from jax.sharding import PartitionSpec as P


RANK = 16
SEND = jnp.float16
PAD = 8
F32 = jnp.float32
BF16 = jnp.bfloat16
GROUPS = ((3,), (2,), (1, 0))


def cost(flops, bytes_accessed):
    return pl.CostEstimate(flops=int(flops), bytes_accessed=int(bytes_accessed), transcendentals=0)


def factor_part(slots, scal, s_ref, a_ref, *rest):
    q_refs, rest, held = rest[: 2 * slots], rest[2 * slots : -1], rest[-1]
    share = q_refs[0].shape[1]
    for j, f_ref in enumerate((s_ref, a_ref)):

        @pl.when(pl.program_id(0) == j)
        def _(f_ref=f_ref, q_refs=q_refs[j * slots : (j + 1) * slots]):
            for i, q_ref in enumerate(q_refs):
                held[:, i * share : (i + 1) * share] = q_ref[...]
            value = jnp.dot(f_ref[...], held[...], preferred_element_type=F32)
            if len(rest) == 1:
                rest[0][0] = value
            else:
                spread(scal, value, *rest)


def spread(scal, value, got_ref, *rest):
    outs, total = rest[:-1], rest[-1]
    value += got_ref[0]
    top = jnp.max(jnp.abs(value), axis=(0, 1), keepdims=True) * (1.0 / 30000.0)
    root = jnp.sqrt(jnp.sqrt(jnp.maximum(top, 2.0**-52))).astype(BF16).astype(F32)
    scale = 1.0 / (root * root * root * root)
    total[...] = value
    rows = outs[0].shape[1]
    chips = value.shape[0] // rows
    at = 0
    for group in range(len(outs) // chips):
        cols = outs[group * chips].shape[2]
        for m in range(chips):
            out = outs[group * chips + m]
            share = total[pl.ds(pl.multiple_of((scal[1] ^ m) * rows, rows), rows), at : at + cols]
            if m:
                out[0, :rows] = share * scale
                out[0, rows:] = jnp.broadcast_to(root, (PAD, cols))
            else:
                out[0] = share
        at += cols


def factor_call(scal, factors, queries, got, keep, masks, rows, share, outs):
    depth = factors[0].shape[1]
    slots = len(masks)
    cols = slots * share
    half = lambda sc: sc[0] if keep else 1 - sc[0]
    in_specs = [pl.BlockSpec((rows, depth), lambda j, sc: (half(sc), 0))] * 2
    for _ in queries:
        for mask in masks:
            in_specs.append(pl.BlockSpec((depth, share), lambda j, sc, mask=mask: (0, sc[2] ^ mask)))
    operands = [*factors, *[q for q in queries for _ in masks]]
    scratch = [pltpu.VMEM((depth, cols), BF16)]
    if keep:
        in_specs.append(pl.BlockSpec((1, rows, cols), lambda j, sc: (j, 0, 0)))
        operands.append(got)
        scratch.insert(0, pltpu.VMEM((rows, cols), F32))
    return pl.pallas_call(
        functools.partial(factor_part, slots),
        out_shape=outs,
        grid_spec=pltpu.PrefetchScalarGridSpec(
            num_scalar_prefetch=1,
            grid=(2,),
            in_specs=in_specs,
            out_specs=[pl.BlockSpec((1, *o.shape[1:]), lambda j, sc: (j, 0, 0)) for o in outs],
            scratch_shapes=scratch,
        ),
        compiler_params=pltpu.CompilerParams(dimension_semantics=("arbitrary",), vmem_limit_bytes=24 << 20),
        cost_estimate=cost(4 * rows * depth * cols, 4 * rows * depth + 4 * depth * cols + 8 * rows * cols),
    )(scal, *operands)


def project(chips, scal, g_ref, a_ref, *rest):
    blocks, outs, held = rest[: 2 * chips], rest[2 * chips : -1], rest[-1]
    rows = blocks[0].shape[1]
    core, chip = scal[0], scal[1]

    @pl.when(pl.program_id(1) == 0)
    def _():
        for m in range(chips):
            at = (chip ^ m) * rows
            for half, block in ((core, blocks[m]), (1 - core, blocks[chips + m])):
                held[pl.ds(pl.multiple_of(half * (chips * rows) + at, rows), rows), :] = block[0]

    for j, tokens_ref in enumerate((g_ref, a_ref)):

        @pl.when(pl.program_id(0) == j)
        def _(tokens_ref=tokens_ref):
            value = jnp.dot(tokens_ref[...], held[...], preferred_element_type=F32)
            at = 0
            for out in outs:
                out[0] = value[:, at : at + out.shape[2]].astype(out.dtype)
                at += out.shape[2]


def tile_of(count):
    return count // 2 if count % 256 == 0 else count


def project_call(scal, tokens, blocks, share, out_types):
    count, feats = tokens[0].shape
    chips, (_, rows, cols) = len(blocks) // 2, blocks[0].shape
    tile = tile_of(count)
    steps = count // tile
    in_specs = [
        pl.BlockSpec((tile, feats), lambda j, t, sc: (jnp.where(j == 0, t, steps - 1), 0)),
        pl.BlockSpec((tile, feats), lambda j, t, sc: (jnp.where(j == 1, t, 0), 0)),
        *[pl.BlockSpec((1, rows, cols), lambda j, t, sc: (j, 0, 0)) for _ in blocks],
    ]
    return pl.pallas_call(
        functools.partial(project, chips),
        out_shape=[jax.ShapeDtypeStruct((2, count, share), t) for t in out_types],
        grid_spec=pltpu.PrefetchScalarGridSpec(
            num_scalar_prefetch=1,
            grid=(2, steps),
            in_specs=in_specs,
            out_specs=[pl.BlockSpec((1, tile, share), lambda j, t, sc: (j, t, 0)) for _ in out_types],
            scratch_shapes=[pltpu.VMEM((feats, cols), BF16)],
        ),
        compiler_params=pltpu.CompilerParams(dimension_semantics=("arbitrary", "arbitrary"), vmem_limit_bytes=24 << 20),
        cost_estimate=cost(4 * count * feats * cols, 4 * count * feats + 4 * feats * cols),
    )(scal, *tokens, *blocks)


def score(*refs):
    parts, out_ref = refs[:-1], refs[-1]
    grads, acts = (sum(p[j].astype(F32) for p in parts) for j in range(2))
    turned = (grads * acts).T
    out_ref[...] = turned.reshape(out_ref.shape[0], RANK, turned.shape[1]).sum(axis=1) * (1.0 / RANK**0.5)


def score_call(*parts):
    _, count, share = parts[0].shape
    tile = tile_of(count)
    return pl.pallas_call(
        score,
        out_shape=jax.ShapeDtypeStruct((share // RANK, count), F32),
        grid=(count // tile,),
        in_specs=[pl.BlockSpec((2, tile, share), lambda t: (0, t, 0))] * len(parts),
        out_specs=pl.BlockSpec((share // RANK, tile), lambda t: (0, t)),
        compiler_params=pltpu.CompilerParams(vmem_limit_bytes=24 << 20),
        cost_estimate=cost(16 * count * share, 16 * count * share),
    )(*parts)


def by_collectives(out_grads, acts, s_inverse, a_inverse, query_out, query_in):
    group = ("tok", "pb")
    projected = []
    for tokens, factor, query in ((out_grads, s_inverse, query_out), (acts, a_inverse, query_in)):
        part = jnp.dot(factor, query, preferred_element_type=F32)
        rows = lax.psum_scatter(part, group, scatter_dimension=0, tiled=True).astype(BF16)
        block = lax.all_gather(rows, group, axis=0, tiled=True)
        part = jnp.dot(tokens, block, preferred_element_type=F32)
        projected.append(lax.psum_scatter(part, "feat", scatter_dimension=1, tiled=True))
    count, share = projected[0].shape
    summed = (projected[0] * projected[1]).reshape(count, share // RANK, RANK).sum(axis=2)
    return (summed * (1.0 / RANK**0.5)).T


def by_transfers(out_grads, acts, s_inverse, a_inverse, query_out, query_in):
    group = ("tok", "pb")
    size, planes = lax.axis_size(group), lax.axis_size("feat")
    at, plane = lax.axis_index(group), lax.axis_index("feat")
    chips, rows, share = size // 2, s_inverse.shape[0] // size, query_out.shape[1] // planes
    table = np.asarray([(i % 2, i // 2, z) for i in range(size) for z in range(planes)], np.int32)
    scal = lax.dynamic_index_in_dim(jnp.asarray(table), at * planes + plane, keepdims=False)
    factors, queries, tokens = (s_inverse, a_inverse), (query_out, query_in), (out_grads, acts)
    half = chips * rows

    def swap(v, m):
        return lax.ppermute(v, group, [(i, i ^ m) for i in range(size)])

    def hop(v, pairs):
        return lax.ppermute(v, "feat", pairs)

    def sent(masks):
        out = jax.ShapeDtypeStruct((2, half, len(masks) * share), F32)
        return factor_call(scal, factors, queries, None, False, masks, half, share, [out])[0]

    def kept(got, groups):
        masks = sum(groups, ())
        outs = [
            jax.ShapeDtypeStruct((2, rows + (PAD if m else 0), len(g) * share), F32) for g in groups for m in range(chips)
        ]
        outs = factor_call(scal, factors, queries, got, True, masks, half, share, outs)
        return [outs[i * chips : (i + 1) * chips] for i in range(len(groups))]

    def reduced(parts):
        total = parts[0]
        for m in range(1, chips):
            got = swap(parts[m].astype(SEND), 2 * m).astype(F32)
            total = total + got[:, :rows] * got[:, rows : rows + 1] ** 4
        return total.astype(BF16)

    def gathered(total):
        mine = [total, *[swap(total, 2 * m) for m in range(1, chips)]]
        return [*mine, *[swap(v, 1) for v in mine]]

    def projected(blocks, types):
        return project_call(scal, tokens, blocks, share, types)

    first, second, third = GROUPS
    sent_ab = sent(first + second)
    got_ab = swap(sent_ab, 1)
    sent_c = sent(third)
    got_c = swap(sent_c, 1)
    parts_a, parts_b = kept(got_ab, (first, second))
    (parts_c,) = kept(got_c, (third,))
    blocks_a = gathered(reduced(parts_a))
    blocks_b = gathered(reduced(parts_b))
    blocks_c = gathered(reduced(parts_c))

    (near,) = projected(blocks_a, (BF16,))
    right = hop(near, [(0, 1), (1, 2)])
    left = hop(near, [(3, 2), (2, 1)])
    (far,) = projected(blocks_b, (F32,))
    on_right, on_left = jnp.where(plane == 1, right, 0), jnp.where(plane == 2, left, 0)
    far = (far + on_right.astype(F32) + on_left.astype(F32)).astype(BF16)
    far = hop(far, [(0, 2), (1, 3), (2, 0), (3, 1)])
    mine = jnp.where(plane == 1, left, 0) + jnp.where(plane == 2, right, 0)
    side, own = projected(blocks_c, (BF16, F32))
    side = hop(side, [(0, 1), (1, 0), (2, 3), (3, 2)])
    return score_call(own, mine, side, far)


def solution(mesh):
    placed = (
        P(("tok", "pb"), "feat"),
        P(("tok", "pb"), "feat"),
        P("feat", ("tok", "pb")),
        P("feat", ("tok", "pb")),
        P(("tok", "pb"), None),
        P(("tok", "pb"), None),
    )

    chips, planes = mesh.shape["tok"] * mesh.shape["pb"] // 2, mesh.shape["feat"]
    direct = chips == 4 and planes == 4

    def per_device(*args):
        return by_transfers(*args) if direct else by_collectives(*args)

    return jax.shard_map(
        per_device, mesh=mesh, in_specs=placed, out_specs=P("feat", ("tok", "pb")), check_vma=False
    )
```
